32 devices in a mesh: expert: 4 (over y, core), dp: 8 (over z, x).
Axes of the slice: x: 2, y: 2, z: 4, core: 2. Of those that a mesh axis runs over, the one named last changes fastest.
Arguments:
- tokens: bfloat16 [512, 4096], P(('expert', 'dp')), may hold values from -6 to 6
- routes: int32 [512, 2], P(('expert', 'dp')), may hold values from 0 to 3, all different within a row; in each aligned block of 16 rows (0 to 15, 16 to 31, ...) at most 12 rows name the same one
- router_logits: float32 [512, 2], P(('expert', 'dp')), may hold values from -0.6 to 0.6
- gate_weight: bfloat16 [4, 4096, 12288], P('expert', None, 'dp'), may hold values from -0.09375 to 0.09375
- up_weight: bfloat16 [4, 4096, 12288], P('expert', None, 'dp'), may hold values from -0.09375 to 0.09375
- down_weight: bfloat16 [4, 12288, 4096], P('expert', 'dp'), may hold values from -0.0546875 to 0.0546875
Outputs:
- mixed_out: bfloat16 [512, 4096], P(('expert', 'dp'))
The draws below stay inside these ranges and needn't reach their ends.
Inputs may be any that keep to these rules, and one draw needn't show every extreme that they name: `routes`: each token names 2 different experts; among the tokens of one device no expert is named more than 12 times, a bound that some block reaches.
All inputs are finite; a program needn't handle non-finite values.
Results may differ from the reference program's by a relative error of at most 0.014.
Values may be sent and summed in bfloat16 or wider, within the bound.
A program may use at most 128 MiB of HBM per device.

```python
import math
import jax
import jax.numpy as jnp
import numpy as np
from jax import lax

D = 4096
FF = 12288
TOPK = 2
TOK_DEV = 16
EXPERTS = 4
TOKENS = 512
C = 12
FFS = 1536
N_EXPERT = 4
N_DP = 8


def level_of(stream_key, dims, cuts, smallest, high):
    def one(axis_at, blocks):
        steps = jax.random.uniform(jax.random.fold_in(jax.random.fold_in(stream_key, 6), axis_at), (blocks,), jnp.float32, smallest / len(cuts), high / len(cuts))
        return jnp.repeat(jnp.exp(steps), dims[axis_at] // blocks).reshape((-1,) + (1,) * (len(dims) - axis_at - 1))

    loudness = one(*cuts[0])
    for cut in cuts[1:]:
        loudness = loudness * one(*cut)
    return loudness


def assign_block(own_key, own, number, rows, count, top, bound, slope):
    sequence = jax.random.permutation(own_key, count)
    crowded, ordinary = portions_of(count, rows * top, bound, slope, True), portions_of(count, rows * top, bound, slope, False)
    places = jnp.arange(count)

    def named(sizes, turn):
        used = int((sizes > 0).sum())
        fixed = max(1, used // 4)
        moved = fixed + (places - fixed + turn * (used - fixed)) % max(1, count - fixed)
        return jnp.zeros((count,), jnp.int32).at[sequence[jnp.where(places < fixed, places, moved)]].set(jnp.asarray(sizes, jnp.int32))

    sizes = jnp.where(number % 4 == 0, named(crowded, number // 4), named(ordinary, number - number // 4 - 1))
    mixed = jax.random.permutation(jax.random.fold_in(own, 3), count)
    source_of, receiver = mixed[0:count // 2 * 2:2], mixed[1:count // 2 * 2:2]
    margin = jnp.minimum(sizes[source_of] - 1, bound - sizes[receiver]) // 2
    margin = jnp.where((source_of == sequence[0]) | (receiver == sequence[0]) | (sizes[receiver] == 0), 0, jnp.maximum(margin, 0))
    moved = jax.random.randint(jax.random.fold_in(own, 4), (count // 2,), 0, 1 << 20) % (margin + 1)
    sizes = sizes.at[source_of].add(-moved).at[receiver].add(moved)
    items = jnp.searchsorted(jnp.cumsum(sizes), jnp.arange(rows * top), side="right").astype(jnp.int32)
    table = items.reshape(top, rows).T
    table = table[jax.random.permutation(jax.random.fold_in(own, 1), rows)]
    turn = jax.random.randint(jax.random.fold_in(own, 2), (rows, 1), 0, top)
    return jnp.take_along_axis(table, (jnp.arange(top)[None, :] + turn) % top, axis=1)


def portions_of(amount, total, most, slope, full):
    portions = [(1 << 20) // math.isqrt(grade ** slope) + 1 for grade in range(1, amount + 1)]
    largest = most if full else min(most, max(-(-total // amount), total * portions[0] // sum(portions)))
    least = 1 if total - largest >= amount - 1 else 0
    counts, spare = [largest] + [least] * (amount - 1), total - largest - least * (amount - 1)
    while spare > 0:
        movable = [i for i in range(1, amount) if counts[i] < largest] or [i for i in range(1, amount) if counts[i] < most]
        whole, budget = sum([portions[i] for i in movable]), spare
        for i in movable:
            extra = min(most - counts[i], max(1, budget * portions[i] // whole), spare)
            counts[i] = counts[i] + extra
            spare = spare - extra
    return np.array(counts)


def normal_values(own_key, extent, scale, most, cuts=(), held_as=jnp.bfloat16):
    values = scale * jax.random.normal(own_key, extent, jnp.float32)
    if cuts:
        values = values * level_of(own_key, extent, cuts, -0.22, 0.18)
    return jnp.clip(values, -most, most).astype(held_as)


def setup_inputs(seed: int = 0) -> dict:
    arg_keys = jax.random.split(jax.random.key(seed), 7)
    tokens = normal_values(arg_keys[0], (TOKENS, D), 1.0, 6.0, ((0, 32),))
    routes_keys = jax.random.split(jax.random.fold_in(arg_keys[1], 1), TOKENS // TOK_DEV)
    routes_turns = jax.random.permutation(jax.random.fold_in(arg_keys[1], 3), TOKENS // TOK_DEV)
    routes = jax.vmap(lambda own, number: assign_block(jax.random.fold_in(arg_keys[1], 2), own, number, TOK_DEV, EXPERTS, TOPK, C, 1))(routes_keys, routes_turns).reshape((TOKENS, TOPK))
    router_logits = jnp.clip(jax.random.uniform(arg_keys[2], (TOKENS, TOPK), jnp.float32, -0.6, 0.6) * level_of(arg_keys[2], (TOKENS, TOPK), ((0, 32),), -0.4, 0.0), -0.6, 0.6)
    gate_weight = normal_values(arg_keys[3], (EXPERTS, D, FF), D ** -0.5, 0.09375, ((0, 4), (2, 8)))
    up_weight = normal_values(arg_keys[4], (EXPERTS, D, FF), D ** -0.5, 0.09375, ((0, 4), (2, 8)))
    down_weight = normal_values(arg_keys[5], (EXPERTS, FF, D), FF ** -0.5, 0.0546875, ((0, 4), (1, 8)))
    return {"tokens": tokens, "routes": routes, "router_logits": router_logits, "gate_weight": gate_weight, "up_weight": up_weight, "down_weight": down_weight}


def reference(tokens, routes, router_logits, gate_weight, up_weight, down_weight):
    shards = N_EXPERT * N_DP
    assigned = routes.reshape(shards, TOK_DEV * TOPK).astype(jnp.int32)
    onehot = (assigned[:, :, None] == jnp.arange(EXPERTS, dtype=jnp.int32)[None, None, :]).astype(jnp.int32)
    earlier = (jnp.cumsum(onehot, axis=1) - onehot).astype(jnp.int32)
    slot_index = jnp.sum(earlier * onehot, axis=2).astype(jnp.int32)
    row_slot = (jnp.arange(shards, dtype=jnp.int32)[:, None] * C + slot_index).astype(jnp.int32)
    copies = jnp.repeat(tokens.reshape(shards, TOK_DEV, D), TOPK, axis=1)
    buffers = jnp.zeros((EXPERTS, shards * C, D), jnp.bfloat16).at[assigned, row_slot].set(copies)

    def run_expert(operands):
        expert_rows, w_gate, w_up, w_down = operands
        gate_proj = jnp.dot(expert_rows, w_gate, preferred_element_type=jnp.float32)
        up_proj = jnp.dot(expert_rows, w_up, preferred_element_type=jnp.float32)
        hidden = (jax.nn.silu(gate_proj) * up_proj).astype(jnp.bfloat16)
        pieces = hidden.reshape(expert_rows.shape[0], N_DP, FFS).transpose(1, 0, 2)
        down_slices = w_down.reshape(N_DP, FFS, D)

        def add_piece(summed, operand_pair):
            partial_value = jnp.dot(operand_pair[0], operand_pair[1], preferred_element_type=jnp.float32).astype(jnp.bfloat16)
            partial_value = lax.optimization_barrier(partial_value)
            return summed + partial_value.astype(jnp.float32), None

        summed, _ = lax.scan(add_piece, jnp.zeros((expert_rows.shape[0], D), jnp.float32), (pieces, down_slices))
        return summed.astype(jnp.bfloat16)

    outputs = lax.map(run_expert, (buffers, gate_weight, up_weight, down_weight))
    picked = outputs[assigned, row_slot].astype(jnp.float32).reshape(TOKENS, TOPK, D)
    weight_first = jax.nn.sigmoid(router_logits[:, 0] - router_logits[:, 1])
    weight_second = jax.nn.sigmoid(router_logits[:, 1] - router_logits[:, 0])
    weights = jnp.stack([weight_first, weight_second], axis=1)
    return jnp.sum(weights[:, :, None] * picked, axis=1).astype(jnp.bfloat16)
```

```python
import functools

import jax
import jax.numpy as jnp
from jax import lax
from jax.experimental import pallas as pl
from jax.experimental.pallas import tpu as pltpu
from jax.sharding import PartitionSpec as P

TOPK = 2
LANES = 128
MESH = pl.DeviceIdType.MESH


def activate_rows(row_block, w_gate, w_up):
    count_rows = row_block.shape[0]
    step_rows = 256 if count_rows % 256 == 0 else count_rows

    def one_step(segment):
        gate_proj = jnp.dot(segment, w_gate, preferred_element_type=jnp.float32)
        up_proj = jnp.dot(segment, w_up, preferred_element_type=jnp.float32)
        return (jax.nn.silu(gate_proj) * up_proj).astype(jnp.bfloat16)

    stepped = lax.map(
        one_step, row_block.reshape(count_rows // step_rows, step_rows, row_block.shape[1])
    )
    return stepped.reshape(count_rows, w_gate.shape[1])


def on_device(tokens, routes, router_logits, gate_weight, up_weight, down_weight):
    experts = lax.axis_size("expert") * gate_weight.shape[0]
    tok_rows = tokens.shape[0]
    model_width = tokens.shape[1]
    capacity = 3 * tok_rows * TOPK // (2 * experts)
    w_gate = gate_weight[0]
    w_up = up_weight[0]
    w_down = down_weight[0]
    assigned = routes.reshape(-1)
    onehot = (assigned[:, None] == jnp.arange(experts, dtype=jnp.int32)[None, :]).astype(jnp.int32)
    slot_index = jnp.sum((jnp.cumsum(onehot, axis=0) - onehot) * onehot, axis=1)
    position = (assigned * capacity + slot_index).reshape(tok_rows, TOPK)
    columns = jnp.arange(experts * capacity, dtype=jnp.int32)
    placed = position[:, :, None] == columns[None, None, :]
    select = jnp.any(placed, axis=1).astype(jnp.bfloat16)
    buffer = lax.dot_general(
        select, tokens, (((0,), (0,)), ((), ())), preferred_element_type=jnp.float32
    )
    buffer = buffer.astype(jnp.bfloat16).reshape(experts, capacity, model_width)
    weight_first = jax.nn.sigmoid(router_logits[:, 0] - router_logits[:, 1])
    weight_second = jax.nn.sigmoid(router_logits[:, 1] - router_logits[:, 0])
    combine = weight_first[:, None] * placed[:, 0, :].astype(jnp.float32) + weight_second[
        :, None
    ] * placed[:, 1, :].astype(jnp.float32)
    received = lax.all_to_all(buffer, "expert", split_axis=0, concat_axis=0, tiled=True)
    sectioned = activate_rows(
        lax.all_gather(received.reshape(-1, model_width), "dp", axis=0, tiled=True), w_gate, w_up
    )
    expert_sum = lax.psum_scatter(
        jnp.dot(sectioned, w_down, preferred_element_type=jnp.float32).astype(jnp.bfloat16),
        "dp",
        scatter_dimension=0,
        tiled=True,
    )
    expert_out = expert_sum.reshape(experts, capacity, model_width)
    returned = lax.all_to_all(
        expert_out, "expert", split_axis=0, concat_axis=0, tiled=True
    ).reshape(-1, model_width)
    mixed_out = jnp.dot(
        combine,
        returned.astype(jnp.float32),
        precision=lax.Precision.HIGHEST,
        preferred_element_type=jnp.float32,
    )
    return mixed_out.astype(jnp.bfloat16)


ZS = 4


def fused_kernel(
    n_ch, toks, routes, logits, gate, up, down, out,
    xg, wg, wu, wd, acc_g, acc_u, hid, part, r0, r1, r2, r3,
    wsem, zs, zr, fs, fr, ss, sr, bs, br, bs2, br2, ss2, sr2, fs2, fr2, zs2, zr2,
):
    rows, width = toks.shape
    ffs = hid.shape[1]
    experts = lax.axis_size("expert")
    total = 8 * ZS * rows
    ck = width // n_ch
    ei = lax.axis_index("expert")
    di = lax.axis_index("dp")
    y = lax.div(ei, 2)
    core = ei - 2 * y
    z = lax.div(di, 2)
    x = di - 2 * z
    f = x + core * (y - x)
    s = y + core * (x - y)
    sib = (ei + 1 - 2 * core, di)
    first = (ei + core * (2 - 4 * y), di + (1 - core) * (1 - 2 * x))
    second = (ei + (1 - core) * (2 - 4 * y), di + core * (1 - 2 * x))
    zpos = [lax.rem(z + j, ZS) for j in range(1, ZS)]
    zdev = [(ei, 2 * p + x) for p in zpos]

    def weight_copy(k, c):
        if k < 2:
            src = (gate, up)[k].at[0, pl.ds(c * ck, ck), :]
            dst = (wg, wu)[k].at[c]
        else:
            src = down.at[0, :, pl.ds(c * ck, ck)]
            dst = wd.at[c]
        return pltpu.make_async_copy(src, dst, wsem.at[k, c])

    for c in range(n_ch):
        weight_copy(0, c).start()
        weight_copy(1, c).start()
    for c in range(n_ch):
        weight_copy(2, c).start()

    lane = lax.broadcasted_iota(jnp.int32, (rows, LANES), 1)
    slot = jnp.where(lane < experts, lane, lane - experts)
    diff = logits[:, 1:2] - logits[:, 0:1]
    w_first = 1.0 / (1.0 + jnp.exp(diff))
    w_second = 1.0 / (1.0 + jnp.exp(-diff))
    weights = jnp.where(slot == routes[:, 0:1], w_first, 0.0) + jnp.where(
        slot == routes[:, 1:2], w_second, 0.0
    )
    high = weights.astype(jnp.bfloat16).astype(jnp.float32)
    coded = jnp.where(lane < experts, high, jnp.where(lane < 2 * experts, weights - high, 0.0))
    xg[core, s, f, z, :, 0:width] = toks[...]
    xg[core, s, f, z, :, width : width + LANES] = coded.astype(jnp.bfloat16)

    barrier = pltpu.get_barrier_semaphore()
    partners = [sib, first, second] + zdev
    for dev in partners:
        pl.semaphore_signal(barrier, inc=1, device_id=dev, device_id_type=MESH)
    pl.semaphore_wait(barrier, len(partners))

    def send(src, dst, s_sem, r_sem, dev):
        return pltpu.make_async_remote_copy(
            src_ref=src, dst_ref=dst, send_sem=s_sem, recv_sem=r_sem,
            device_id=dev, device_id_type=MESH,
        )

    def cols(c):
        return pl.ds(c * ck, ck + (LANES if c == n_ch - 1 else 0))

    ag_z, ag_f, ag_s, ag_b = [], [], [], []
    for c in range(n_ch):
        v = xg.at[core, s, f, z, :, cols(c)]
        ag_z.append([send(v, v, zs.at[c, j], zr.at[c, j], zdev[j]) for j in range(ZS - 1)])
        v = xg.at[core, s, f, :, :, cols(c)]
        ag_f.append(send(v, v, fs.at[c], fr.at[c], first))
        v = xg.at[core, s, :, :, :, cols(c)]
        ag_s.append(send(v, v, ss.at[c], sr.at[c], second))
        v = xg.at[core, :, :, :, :, cols(c)]
        ag_b.append(send(v, v, bs.at[c], br.at[c], sib))

    nt = 512 if ffs % 512 == 0 else ffs
    dn = 512 if ck % 512 == 0 else ck

    def up_chunk(c):
        weight_copy(0, c).wait()
        weight_copy(1, c).wait()
        last = c == n_ch - 1
        if last:
            sel = lax.broadcasted_iota(jnp.int32, (total, LANES), 1)
            coded_all = xg[:, :, :, :, :, width : width + LANES].reshape(total, LANES)
            mine = (sel == ei) | (sel == ei + experts)
            w_row = jnp.sum(
                jnp.where(mine, coded_all.astype(jnp.float32), 0.0), axis=1, keepdims=True
            )

        def tile(i, carry):
            at = pl.ds(pl.multiple_of(i * nt, nt), nt)
            xs = xg[:, :, :, :, :, c * ck : (c + 1) * ck].reshape(total, ck)
            g = jnp.dot(xs, wg[c, :, at], preferred_element_type=jnp.float32)
            u = jnp.dot(xs, wu[c, :, at], preferred_element_type=jnp.float32)
            if c > 0:
                g = acc_g[:, at] + g
                u = acc_u[:, at] + u
            if last:
                act = g / (1.0 + jnp.exp(-g)) * u * w_row
                hid[:, at] = act.astype(jnp.bfloat16)
            else:
                acc_g[:, at] = g
                acc_u[:, at] = u
            return carry

        lax.fori_loop(0, ffs // nt, tile, 0)

    for cp in ag_z[0]:
        cp.start()
    for t in range(n_ch + 3):
        if t < n_ch:
            for cp in ag_z[t]:
                cp.wait_recv()
            ag_f[t].start()
            if t + 1 < n_ch:
                for cp in ag_z[t + 1]:
                    cp.start()
        if 0 <= t - 1 < n_ch:
            ag_f[t - 1].wait_recv()
            ag_s[t - 1].start()
        if 0 <= t - 2 < n_ch:
            ag_s[t - 2].wait_recv()
            ag_b[t - 2].start()
        if 0 <= t - 3 < n_ch:
            ag_b[t - 3].wait_recv()
            up_chunk(t - 3)

    other = 1 - core
    rs_b, rs_s, rs_f, rs_z = [], [], [], []
    for c in range(n_ch):
        at = pl.ds(c * ck, ck)
        rs_b.append(
            send(part.at[other, :, :, :, :, at], r0.at[:, :, :, :, at], bs2.at[c], br2.at[c], sib)
        )
        rs_s.append(
            send(part.at[core, 1 - s, :, :, :, at], r1.at[:, :, :, at], ss2.at[c], sr2.at[c], second)
        )
        rs_f.append(
            send(part.at[core, s, 1 - f, :, :, at], r2.at[:, :, at], fs2.at[c], fr2.at[c], first)
        )
        rs_z.append(
            [
                send(
                    part.at[core, s, f, zpos[j], :, at], r3.at[j, :, at],
                    zs2.at[c, j], zr2.at[c, j], zdev[j],
                )
                for j in range(ZS - 1)
            ]
        )

    def f32(v):
        return v.astype(jnp.float32)

    def down_chunk(c):
        weight_copy(2, c).wait()

        for i in range(ck // dn):
            res = jnp.dot(
                hid[...], wd[c, :, i * dn : (i + 1) * dn], preferred_element_type=jnp.float32
            )
            lo = c * ck + i * dn
            part[:, :, :, :, :, lo : lo + dn] = res.astype(jnp.bfloat16).reshape(
                2, 2, 2, ZS, rows, dn
            )

    for t in range(n_ch + 4):
        if t < n_ch:
            down_chunk(t)
            rs_b[t].start()
        if 0 <= t - 1 < n_ch:
            c = t - 1
            at = pl.ds(c * ck, ck)
            rs_b[c].wait_recv()
            part[core, 1 - s, :, :, :, at] = (
                f32(part[core, 1 - s, :, :, :, at]) + f32(r0[1 - s, :, :, :, at])
            ).astype(jnp.bfloat16)
            rs_s[c].start()
        if 0 <= t - 2 < n_ch:
            c = t - 2
            at = pl.ds(c * ck, ck)
            rs_s[c].wait_recv()
            part[core, s, 1 - f, :, :, at] = (
                f32(part[core, s, 1 - f, :, :, at])
                + f32(r0[s, 1 - f, :, :, at])
                + f32(r1[1 - f, :, :, at])
            ).astype(jnp.bfloat16)
            rs_f[c].start()
        if 0 <= t - 3 < n_ch:
            c = t - 3
            at = pl.ds(c * ck, ck)
            rs_f[c].wait_recv()
            part[core, s, f, :, :, at] = (
                f32(part[core, s, f, :, :, at])
                + f32(r0[s, f, :, :, at])
                + f32(r1[f, :, :, at])
                + f32(r2[:, :, at])
            ).astype(jnp.bfloat16)
            for cp in rs_z[c]:
                cp.start()
        if 0 <= t - 4 < n_ch:
            c = t - 4
            at = pl.ds(c * ck, ck)
            for cp in rs_z[c]:
                cp.wait_recv()
            out[:, at] = (
                f32(part[core, s, f, z, :, at])
                + f32(r3[0, :, at])
                + f32(r3[1, :, at])
                + f32(r3[2, :, at])
            ).astype(jnp.bfloat16)

    for c in range(n_ch):
        for cp in ag_z[c] + [ag_f[c], ag_s[c], ag_b[c], rs_b[c], rs_s[c], rs_f[c]] + rs_z[c]:
            cp.wait_send()


def fused_device(tokens, routes, router_logits, gate_weight, up_weight, down_weight):
    rows, width = tokens.shape
    ffs = gate_weight.shape[2]
    n_ch = 4
    ck = width // n_ch
    total = 8 * ZS * rows
    bf = jnp.bfloat16
    dma = pltpu.SemaphoreType.DMA
    vmem = pl.BlockSpec(memory_space=pltpu.VMEM)
    hbm = pl.BlockSpec(memory_space=pl.ANY)
    flops = 6 * total * width * ffs
    one = dma((n_ch,))
    three = dma((n_ch, ZS - 1))
    return pl.pallas_call(
        functools.partial(fused_kernel, n_ch),
        out_shape=jax.ShapeDtypeStruct((rows, width), bf),
        in_specs=[vmem, vmem, vmem, hbm, hbm, hbm],
        out_specs=vmem,
        scratch_shapes=[
            pltpu.VMEM((2, 2, 2, ZS, rows, width + LANES), bf),
            pltpu.VMEM((n_ch, ck, ffs), bf),
            pltpu.VMEM((n_ch, ck, ffs), bf),
            pltpu.VMEM((n_ch, ffs, ck), bf),
            pltpu.VMEM((total, ffs), jnp.float32),
            pltpu.VMEM((total, ffs), jnp.float32),
            pltpu.VMEM((total, ffs), bf),
            pltpu.VMEM((2, 2, 2, ZS, rows, width), bf),
            pltpu.VMEM((2, 2, ZS, rows, width), bf),
            pltpu.VMEM((2, ZS, rows, width), bf),
            pltpu.VMEM((ZS, rows, width), bf),
            pltpu.VMEM((ZS - 1, rows, width), bf),
            dma((3, n_ch)),
            three, three, one, one, one, one, one, one,
            one, one, one, one, one, one, three, three,
        ],
        compiler_params=pltpu.CompilerParams(
            collective_id=0, has_side_effects=True, vmem_limit_bytes=62 * 2**20
        ),
        cost_estimate=pl.CostEstimate(
            flops=flops, bytes_accessed=6 * width * ffs, transcendentals=total * ffs
        ),
        name="moe_fused",
    )(tokens, routes, router_logits, gate_weight, up_weight, down_weight)


def solution(mesh):
    placed = (
        P(("expert", "dp"), None),
        P(("expert", "dp"), None),
        P(("expert", "dp"), None),
        P("expert", None, "dp"),
        P("expert", None, "dp"),
        P("expert", "dp", None),
    )
    small = mesh.shape["expert"] == 4 and mesh.shape["dp"] == 2 * ZS
    return jax.shard_map(
        fused_device if small else on_device,
        mesh=mesh,
        in_specs=placed,
        out_specs=P(("expert", "dp"), None),
        check_vma=False,
    )
```

```python
import functools

import jax
import jax.numpy as jnp
from jax import lax
from jax.experimental import pallas as pl
from jax.experimental.pallas import tpu as pltpu
from jax.sharding import PartitionSpec as P

TOPK = 2
LANES = 128
MESH = pl.DeviceIdType.MESH


def activate_rows(row_block, w_gate, w_up):
    count_rows = row_block.shape[0]
    step_rows = 256 if count_rows % 256 == 0 else count_rows

    def one_step(segment):
        gate_proj = jnp.dot(segment, w_gate, preferred_element_type=jnp.float32)
        up_proj = jnp.dot(segment, w_up, preferred_element_type=jnp.float32)
        return (jax.nn.silu(gate_proj) * up_proj).astype(jnp.bfloat16)

    stepped = lax.map(
        one_step, row_block.reshape(count_rows // step_rows, step_rows, row_block.shape[1])
    )
    return stepped.reshape(count_rows, w_gate.shape[1])


def on_device(tokens, routes, router_logits, gate_weight, up_weight, down_weight):
    experts = lax.axis_size("expert") * gate_weight.shape[0]
    tok_rows = tokens.shape[0]
    model_width = tokens.shape[1]
    capacity = 3 * tok_rows * TOPK // (2 * experts)
    w_gate = gate_weight[0]
    w_up = up_weight[0]
    w_down = down_weight[0]
    assigned = routes.reshape(-1)
    onehot = (assigned[:, None] == jnp.arange(experts, dtype=jnp.int32)[None, :]).astype(jnp.int32)
    slot_index = jnp.sum((jnp.cumsum(onehot, axis=0) - onehot) * onehot, axis=1)
    position = (assigned * capacity + slot_index).reshape(tok_rows, TOPK)
    columns = jnp.arange(experts * capacity, dtype=jnp.int32)
    placed = position[:, :, None] == columns[None, None, :]
    select = jnp.any(placed, axis=1).astype(jnp.bfloat16)
    buffer = lax.dot_general(
        select, tokens, (((0,), (0,)), ((), ())), preferred_element_type=jnp.float32
    )
    buffer = buffer.astype(jnp.bfloat16).reshape(experts, capacity, model_width)
    weight_first = jax.nn.sigmoid(router_logits[:, 0] - router_logits[:, 1])
    weight_second = jax.nn.sigmoid(router_logits[:, 1] - router_logits[:, 0])
    combine = weight_first[:, None] * placed[:, 0, :].astype(jnp.float32) + weight_second[
        :, None
    ] * placed[:, 1, :].astype(jnp.float32)
    received = lax.all_to_all(buffer, "expert", split_axis=0, concat_axis=0, tiled=True)
    sectioned = activate_rows(
        lax.all_gather(received.reshape(-1, model_width), "dp", axis=0, tiled=True), w_gate, w_up
    )
    expert_sum = lax.psum_scatter(
        jnp.dot(sectioned, w_down, preferred_element_type=jnp.float32).astype(jnp.bfloat16),
        "dp",
        scatter_dimension=0,
        tiled=True,
    )
    expert_out = expert_sum.reshape(experts, capacity, model_width)
    returned = lax.all_to_all(
        expert_out, "expert", split_axis=0, concat_axis=0, tiled=True
    ).reshape(-1, model_width)
    mixed_out = jnp.dot(
        combine,
        returned.astype(jnp.float32),
        precision=lax.Precision.HIGHEST,
        preferred_element_type=jnp.float32,
    )
    return mixed_out.astype(jnp.bfloat16)


ZS = 4


def fused_kernel(
    n_ch, toks, routing, gate, up, down, out,
    xg, wg, wu, wd, acc_g, acc_u, hid, part, r0, r1, r2, r3,
    wsem, zs, zr, fs, fr, ss, sr, bs, br, bs2, br2, ss2, sr2, fs2, fr2, zs2, zr2,
    sbs, sbr, sbs2, sbr2,
):
    rows, width = toks.shape
    ffs = hid.shape[1]
    experts = lax.axis_size("expert")
    total = 8 * ZS * rows
    ck = width // n_ch
    ei = lax.axis_index("expert")
    di = lax.axis_index("dp")
    y = lax.div(ei, 2)
    core = ei - 2 * y
    z = lax.div(di, 2)
    x = di - 2 * z
    f = x + core * (y - x)
    s = y + core * (x - y)
    sib = (ei + 1 - 2 * core, di)
    first = (ei + core * (2 - 4 * y), di + (1 - core) * (1 - 2 * x))
    second = (ei + (1 - core) * (2 - 4 * y), di + core * (1 - 2 * x))
    zpos = [lax.rem(z + j, ZS) for j in range(1, ZS)]
    zdev = [(ei, 2 * p + x) for p in zpos]

    def weight_copy(k, c):
        if k < 2:
            src = (gate, up)[k].at[0, pl.ds(c * ck, ck), :]
            dst = (wg, wu)[k].at[c]
        else:
            src = down.at[0, :, pl.ds(c * ck, ck)]
            dst = wd.at[c]
        return pltpu.make_async_copy(src, dst, wsem.at[k, c])

    for c in range(n_ch):
        weight_copy(0, c).start()
        weight_copy(1, c).start()
    for c in range(n_ch):
        weight_copy(2, c).start()

    lane = lax.broadcasted_iota(jnp.int32, (rows, LANES), 1)
    slot = jnp.where(lane < experts, lane, lane - experts).astype(jnp.float32)
    diff = routing[:, 3:4] - routing[:, 2:3]
    w_first = 1.0 / (1.0 + jnp.exp(diff))
    w_second = 1.0 / (1.0 + jnp.exp(-diff))
    weights = jnp.where(slot == routing[:, 0:1], w_first, 0.0) + jnp.where(
        slot == routing[:, 1:2], w_second, 0.0
    )
    high = weights.astype(jnp.bfloat16).astype(jnp.float32)
    coded = jnp.where(lane < experts, high, jnp.where(lane < 2 * experts, weights - high, 0.0))
    xg[core, s, f, z, :, 0:width] = toks[...]
    xg[core, s, f, z, :, width : width + LANES] = coded.astype(jnp.bfloat16)

    barrier = pltpu.get_barrier_semaphore()
    partners = [sib, first, second] + zdev
    for dev in partners:
        pl.semaphore_signal(barrier, inc=1, device_id=dev, device_id_type=MESH)
    pl.semaphore_wait(barrier, len(partners))

    def send(src, dst, s_sem, r_sem, dev):
        return pltpu.make_async_remote_copy(
            src_ref=src, dst_ref=dst, send_sem=s_sem, recv_sem=r_sem,
            device_id=dev, device_id_type=MESH,
        )

    def cols(c):
        return pl.ds(c * ck, ck + (LANES if c == n_ch - 1 else 0))

    ag_z, ag_f, ag_s, ag_t, ag_b = [], [], [], [], []
    for c in range(n_ch):
        v = xg.at[core, s, f, z, :, cols(c)]
        ag_z.append([send(v, v, zs.at[c, j], zr.at[c, j], zdev[j]) for j in range(ZS - 1)])
        v = xg.at[core, s, f, :, :, cols(c)]
        ag_f.append(send(v, v, fs.at[c], fr.at[c], first))
        ag_s.append(send(v, v, ss.at[c], sr.at[c], second))
        v = xg.at[core, s, 1 - f, :, :, cols(c)]
        ag_t.append(send(v, v, sbs.at[c], sbr.at[c], second))
        v = xg.at[core, :, :, :, :, cols(c)]
        ag_b.append(send(v, v, bs.at[c], br.at[c], sib))

    nt = 512 if ffs % 512 == 0 else ffs
    dn = 512 if ck % 512 == 0 else ck

    def up_chunk(c):
        weight_copy(0, c).wait()
        weight_copy(1, c).wait()
        last = c == n_ch - 1
        if last:
            sel = lax.broadcasted_iota(jnp.int32, (total, LANES), 1)
            coded_all = xg[:, :, :, :, :, width : width + LANES].reshape(total, LANES)
            mine = (sel == ei) | (sel == ei + experts)
            w_row = jnp.sum(
                jnp.where(mine, coded_all.astype(jnp.float32), 0.0), axis=1, keepdims=True
            )

        def tile(i, carry):
            at = pl.ds(pl.multiple_of(i * nt, nt), nt)
            xs = xg[:, :, :, :, :, c * ck : (c + 1) * ck].reshape(total, ck)
            g = jnp.dot(xs, wg[c, :, at], preferred_element_type=jnp.float32)
            u = jnp.dot(xs, wu[c, :, at], preferred_element_type=jnp.float32)
            if c > 0:
                g = acc_g[:, at] + g
                u = acc_u[:, at] + u
            if last:
                act = g / (1.0 + jnp.exp(-g)) * u * w_row
                hid[:, at] = act.astype(jnp.bfloat16)
            else:
                acc_g[:, at] = g
                acc_u[:, at] = u
            return carry

        lax.fori_loop(0, ffs // nt, tile, 0)

    for cp in ag_z[0] + ag_z[1]:
        cp.start()
    for t in range(n_ch + 3):
        if t < n_ch:
            for cp in ag_z[t]:
                cp.wait_recv()
            ag_f[t].start()
            ag_s[t].start()
            if t + 2 < n_ch:
                for cp in ag_z[t + 2]:
                    cp.start()
        if 0 <= t - 1 < n_ch:
            ag_f[t - 1].wait_recv()
            ag_t[t - 1].start()
        if 0 <= t - 2 < n_ch:
            ag_s[t - 2].wait_recv()
            ag_t[t - 2].wait_recv()
            ag_b[t - 2].start()
        if 0 <= t - 3 < n_ch:
            ag_b[t - 3].wait_recv()
            up_chunk(t - 3)

    other = 1 - core
    rs_b, rs_s, rs_t, rs_f, rs_z = [], [], [], [], []
    for c in range(n_ch):
        at = pl.ds(c * ck, ck)
        rs_b.append(
            send(part.at[other, :, :, :, :, at], r0.at[:, :, :, :, at], bs2.at[c], br2.at[c], sib)
        )
        rs_s.append(
            send(
                part.at[core, 1 - s, 1 - f, :, :, at], r1.at[1 - f, :, :, at],
                ss2.at[c], sr2.at[c], second,
            )
        )
        rs_t.append(
            send(part.at[core, 1 - s, f, :, :, at], r1.at[f, :, :, at], sbs2.at[c], sbr2.at[c], second)
        )
        rs_f.append(
            send(part.at[core, s, 1 - f, :, :, at], r2.at[:, :, at], fs2.at[c], fr2.at[c], first)
        )
        rs_z.append(
            [
                send(
                    part.at[core, s, f, zpos[j], :, at], r3.at[j, :, at],
                    zs2.at[c, j], zr2.at[c, j], zdev[j],
                )
                for j in range(ZS - 1)
            ]
        )

    def f32(v):
        return v.astype(jnp.float32)

    def down_chunk(c):
        weight_copy(2, c).wait()

        for i in range(ck // dn):
            res = jnp.dot(
                hid[...], wd[c, :, i * dn : (i + 1) * dn], preferred_element_type=jnp.float32
            )
            lo = c * ck + i * dn
            part[:, :, :, :, :, lo : lo + dn] = res.astype(jnp.bfloat16).reshape(
                2, 2, 2, ZS, rows, dn
            )

    for t in range(n_ch + 4):
        if t < n_ch:
            down_chunk(t)
            rs_b[t].start()
        if 0 <= t - 1 < n_ch:
            c = t - 1
            at = pl.ds(c * ck, ck)
            rs_b[c].wait_recv()
            for g, cp in ((1 - f, rs_s[c]), (f, rs_t[c])):
                part[core, 1 - s, g, :, :, at] = (
                    f32(part[core, 1 - s, g, :, :, at]) + f32(r0[1 - s, g, :, :, at])
                ).astype(jnp.bfloat16)
                cp.start()
        if 0 <= t - 2 < n_ch:
            c = t - 2
            at = pl.ds(c * ck, ck)
            rs_s[c].wait_recv()
            part[core, s, 1 - f, :, :, at] = (
                f32(part[core, s, 1 - f, :, :, at])
                + f32(r0[s, 1 - f, :, :, at])
                + f32(r1[1 - f, :, :, at])
            ).astype(jnp.bfloat16)
            rs_f[c].start()
        if 0 <= t - 3 < n_ch:
            c = t - 3
            at = pl.ds(c * ck, ck)
            rs_t[c].wait_recv()
            rs_f[c].wait_recv()
            part[core, s, f, :, :, at] = (
                f32(part[core, s, f, :, :, at])
                + f32(r0[s, f, :, :, at])
                + f32(r1[f, :, :, at])
                + f32(r2[:, :, at])
            ).astype(jnp.bfloat16)
            for cp in rs_z[c]:
                cp.start()
        if 0 <= t - 4 < n_ch:
            c = t - 4
            at = pl.ds(c * ck, ck)
            for cp in rs_z[c]:
                cp.wait_recv()
            out[:, at] = (
                f32(part[core, s, f, z, :, at])
                + f32(r3[0, :, at])
                + f32(r3[1, :, at])
                + f32(r3[2, :, at])
            ).astype(jnp.bfloat16)

    for c in range(n_ch):
        for cp in ag_z[c] + [ag_f[c], ag_s[c], ag_t[c], ag_b[c], rs_b[c], rs_s[c], rs_t[c], rs_f[c]] + rs_z[c]:
            cp.wait_send()


def fused_device(tokens, routes, router_logits, gate_weight, up_weight, down_weight):
    rows, width = tokens.shape
    routing = jnp.concatenate([routes.astype(jnp.float32), router_logits], axis=1)
    ffs = gate_weight.shape[2]
    n_ch = 4
    ck = width // n_ch
    total = 8 * ZS * rows
    bf = jnp.bfloat16
    dma = pltpu.SemaphoreType.DMA
    vmem = pl.BlockSpec(memory_space=pltpu.VMEM)
    hbm = pl.BlockSpec(memory_space=pl.ANY)
    flops = 6 * total * width * ffs
    one = dma((n_ch,))
    three = dma((n_ch, ZS - 1))
    return pl.pallas_call(
        functools.partial(fused_kernel, n_ch),
        out_shape=jax.ShapeDtypeStruct((rows, width), bf),
        in_specs=[vmem, vmem, hbm, hbm, hbm],
        out_specs=vmem,
        scratch_shapes=[
            pltpu.VMEM((2, 2, 2, ZS, rows, width + LANES), bf),
            pltpu.VMEM((n_ch, ck, ffs), bf),
            pltpu.VMEM((n_ch, ck, ffs), bf),
            pltpu.VMEM((n_ch, ffs, ck), bf),
            pltpu.VMEM((total, ffs), jnp.float32),
            pltpu.VMEM((total, ffs), jnp.float32),
            pltpu.VMEM((total, ffs), bf),
            pltpu.VMEM((2, 2, 2, ZS, rows, width), bf),
            pltpu.VMEM((2, 2, ZS, rows, width), bf),
            pltpu.VMEM((2, ZS, rows, width), bf),
            pltpu.VMEM((ZS, rows, width), bf),
            pltpu.VMEM((ZS - 1, rows, width), bf),
            dma((3, n_ch)),
            three, three, one, one, one, one, one, one,
            one, one, one, one, one, one, three, three,
            one, one, one, one,
        ],
        compiler_params=pltpu.CompilerParams(
            collective_id=0, has_side_effects=True, vmem_limit_bytes=62 * 2**20
        ),
        cost_estimate=pl.CostEstimate(
            flops=flops, bytes_accessed=6 * width * ffs, transcendentals=total * ffs
        ),
        name="moe_fused",
    )(tokens, routing, gate_weight, up_weight, down_weight)


def solution(mesh):
    placed = (
        P(("expert", "dp"), None),
        P(("expert", "dp"), None),
        P(("expert", "dp"), None),
        P("expert", None, "dp"),
        P("expert", None, "dp"),
        P("expert", "dp", None),
    )
    small = mesh.shape["expert"] == 4 and mesh.shape["dp"] == 2 * ZS
    return jax.shard_map(
        fused_device if small else on_device,
        mesh=mesh,
        in_specs=placed,
        out_specs=P(("expert", "dp"), None),
        check_vma=False,
    )
```
